128 devices in a mesh: gx: 8 (over z_lo, x), gy: 16 (over y, z_hi, core).
Axes of the slice: x: 4, y: 4, z: 4 (z_hi: 2, z_lo: 2; z = z_hi * 2 + z_lo), core: 2. Of those that a mesh axis runs over, the one named last changes fastest.
Arguments:
- samples: float32 [2048, 512], replicated, may hold values from -1 to 1
- real_idx: int32 [16, 16, 256], P('gx', 'gy'), may hold values from 0 to 2047
- latents: float32 [16, 16, 256, 512], P('gx', 'gy'), may hold values from -6 to 6
- gen_weight: float32 [16, 16, 512, 512], P('gx', 'gy'), may hold values from -6 to 6
- disc_weight: float32 [16, 16, 512, 512], P('gx', 'gy'), may hold values from -6 to 6
- disc_head: float32 [16, 16, 512], P('gx', 'gy'), may hold values from -6 to 6
Outputs:
- new_gen: float32 [16, 16, 512, 512], P('gx', 'gy')
- new_disc: float32 [16, 16, 512, 512], P('gx', 'gy')
- new_head: float32 [16, 16, 512], P('gx', 'gy')
The draws below stay inside these ranges and needn't reach their ends.
All inputs are finite; a program needn't handle non-finite values.
Results may differ from the reference program's by a relative error of at most 0.0001.
Values sent between devices are 32-bit elements; how exact they have to be, the bound alone decides.
No kernel may reach another device: no remote copies, remote signals or barrier semaphores. Data moves between devices by JAX's collectives and lax.ppermute only.
A program may use at most 128 MiB of HBM per device.

```python
import jax
import jax.numpy as jnp
from jax import lax

W = 512
ROWS = 256
TABLE = 2048
NX = 16
NY = 16


def place_ends(entries, own_key, low, top_value):
    longest = entries.shape.index(max(entries.shape))
    spots = []
    for shift in (0, 1):
        where = [jax.random.randint(jax.random.fold_in(own_key, axis), (), 0, length) for axis, length in enumerate(entries.shape)]
        where[longest] = (where[longest] + shift) % entries.shape[longest]
        spots.append(tuple(where))
    return entries.at[spots[0]].set(low).at[spots[1]].set(top_value)


def block_scale(stream_key, shape, pieces, smallest, high):
    level = 1.0
    for dim, parts in pieces:
        heights = jax.random.uniform(jax.random.fold_in(jax.random.fold_in(stream_key, 6), dim), (parts,), jnp.float32, smallest / len(pieces), high / len(pieces))
        level = level * jnp.repeat(jnp.exp(heights), shape[dim] // parts).reshape((-1,) + (1,) * (len(shape) - 1 - dim))
    return level


def bell_draw(stream_key, extent, width, most, pieces=(), held_as=jnp.bfloat16):
    drawn = jax.random.normal(stream_key, extent, jnp.float32) * width
    if len(pieces) > 0:
        drawn = block_scale(stream_key, extent, pieces, -0.22, 0.18) * drawn
    return jnp.clip(drawn, min=-most, max=most).astype(held_as)


def setup_inputs(seed: int = 0) -> dict:
    seeds = jax.random.split(jax.random.key(seed), 7)
    return {
        "samples": jnp.clip(jax.random.uniform(seeds[0], (TABLE, W), jnp.float32, -1.0, 1.0), -1.0, 1.0),
        "real_idx": place_ends(jax.random.randint(seeds[1], (NX, NY, ROWS), 0, TABLE), jax.random.fold_in(seeds[1], 1), 0, TABLE - 1).astype(jnp.int32),
        "latents": bell_draw(seeds[2], (NX, NY, ROWS, W), 1.0, 6.0, ((0, 8), (1, 16)), jnp.float32),
        "gen_weight": bell_draw(seeds[3], (NX, NY, W, W), 1.0, 6.0, ((0, 8), (1, 16)), jnp.float32),
        "disc_weight": bell_draw(seeds[4], (NX, NY, W, W), 1.0, 6.0, ((0, 8), (1, 16)), jnp.float32),
        "disc_head": bell_draw(seeds[5], (NX, NY, W), 1.0, 6.0, ((0, 8), (1, 16)), jnp.float32),
    }


HIGH = lax.Precision.HIGHEST

def product(left, right):
    return jnp.einsum('xybk,xykn->xybn', left, right, precision=HIGH)

def beside_all(field):
    return [field, jnp.roll(field, 1, 0), jnp.roll(field, -1, 0), jnp.roll(field, 1, 1), jnp.roll(field, -1, 1)]

def opponent(fake, weight, head, scale):
    hidden = jnp.tanh(scale * product(fake, weight))
    score = scale * jnp.einsum('xybn,xyn->xyb', hidden, head, precision=HIGH)
    slope = -jax.nn.sigmoid(-score)
    inner = (1.0 - hidden * hidden) * (scale * slope[..., None] * head[:, :, None, :])
    return scale * jnp.einsum('xybn,xykn->xybk', inner, weight, precision=HIGH)

def critic(inputs, weight, head, scale, real_side):
    hidden = jnp.tanh(scale * product(inputs, weight))
    score = scale * jnp.einsum('xybn,xyn->xyb', hidden, head, precision=HIGH)
    if real_side:
        slope = -jax.nn.sigmoid(-score)
    else:
        slope = 0.2 * jax.nn.sigmoid(score)
    inner = (1.0 - hidden * hidden) * (scale * slope[..., None] * head[:, :, None, :])
    grad_w = scale * jnp.einsum('xybk,xybn->xykn', inputs, inner, precision=HIGH)
    grad_h = scale * jnp.einsum('xyb,xybn->xyn', slope, hidden, precision=HIGH)
    return (grad_w, grad_h)

def descend(value, grad, axes):
    mean_sq = lax.optimization_barrier(jnp.mean(grad * grad, axis=axes, keepdims=True))
    return value - 0.25 * grad * lax.rsqrt(mean_sq + 1e-06)

def reference(samples, real_idx, latents, gen_weight, disc_weight, disc_head):
    scale = W ** (-0.5)
    fake = jnp.tanh(scale * product(latents, gen_weight))
    back = jnp.zeros_like(fake)
    for weight, head in zip(beside_all(disc_weight), beside_all(disc_head)):
        back = back + opponent(fake, weight, head, scale)
    gen_grad = scale * jnp.einsum('xybk,xybn->xykn', latents, (1.0 - fake * fake) * back, precision=HIGH)
    new_gen = descend(gen_weight, gen_grad, (2, 3))
    real = jnp.take(samples, real_idx, axis=0)
    grad_w, grad_h = critic(real, disc_weight, disc_head, scale, True)
    for generator in beside_all(new_gen):
        made = jnp.tanh(scale * product(latents, generator))
        term_w, term_h = critic(made, disc_weight, disc_head, scale, False)
        grad_w = grad_w + term_w
        grad_h = grad_h + term_h
    new_disc = descend(disc_weight, grad_w, (2, 3))
    new_head = descend(disc_head, grad_h, (2,))
    return (new_gen, new_disc, new_head)
```

```python
import jax
import jax.numpy as jnp
from jax import lax
from jax.experimental import pallas as pl
from jax.experimental.pallas import tpu as pltpu
from jax.sharding import PartitionSpec as P


RATE = 0.25
PAD = 8


def split(value):
    high = value.astype(jnp.bfloat16)
    low = (value - high.astype(jnp.float32)).astype(jnp.bfloat16)
    return high, low


def dot(left, right, dims):
    def one(a, b):
        return lax.dot_general(
            a, b, ((dims[:1], dims[1:]), ((), ())), preferred_element_type=jnp.float32
        )

    return one(left[0], right[0]) + (one(left[0], right[1]) + one(left[1], right[0]))


def generated(rows, weight, scale):
    return jnp.tanh(scale * dot(rows, weight, (1, 0)))


def opponent(fake, weight, head, scale):
    hidden = jnp.tanh(scale * dot(fake, weight, (1, 0)))
    score = scale * jnp.sum(hidden * head, axis=1, keepdims=True)
    slope = -jax.nn.sigmoid(-score)
    inner = (1.0 - hidden * hidden) * ((scale * slope) * head)
    return scale * dot(split(inner), weight, (1, 1))


def critic(rows, weight, head, scale, real_side):
    rows = split(rows)
    hidden = jnp.tanh(scale * dot(rows, weight, (1, 0)))
    score = scale * jnp.sum(hidden * head, axis=1, keepdims=True)
    if real_side:
        slope = -jax.nn.sigmoid(-score)
    else:
        slope = 0.2 * jax.nn.sigmoid(score)
    inner = (1.0 - hidden * hidden) * ((scale * slope) * head)
    grad_w = scale * dot(rows, split(inner), (0, 0))
    grad_h = scale * jnp.sum(slope * hidden, axis=0, keepdims=True)
    return grad_w, grad_h


def descend(value, grad):
    mean_sq = jnp.mean(grad * grad)
    return value - RATE * grad * lax.rsqrt(mean_sq + 1e-06)


def pack_kernel(weight, head, both, first, last):
    cell = pl.program_id(0)
    width = weight.shape[1]
    filler = jnp.broadcast_to(head[0], (PAD, weight.shape[2]))
    both[0, :width] = weight[0]
    both[0, width:] = filler

    @pl.when(cell == 0)
    def _():
        first[0, :width] = weight[0]
        first[0, width:] = filler

    @pl.when(cell == 1)
    def _():
        last[0, :width] = weight[0]
        last[0, width:] = filler


def start_kernel(scale, rows, gen, weight, head, weight_in, head_in, fake, back):
    value = generated(split(rows[0]), split(gen[0]), scale)
    fake[0] = value
    value = split(value)
    total = opponent(value, split(weight[0]), head[0], scale)
    back[0] = total + opponent(value, split(weight_in[0]), head_in[0], scale)


def packed(ref):
    width = ref.shape[2]
    return split(ref[0, :width]), ref[0, width : width + 1]


def chip_kernel(scale, fake, pack, back, out):
    weight, head = packed(pack)
    out[0] = back[0] + opponent(split(fake[0]), weight, head, scale)


def chosen(low, high):
    cell = pl.program_id(0)
    return jnp.where(cell == 0, low[...], high[...])


def outer_kernel(scale, fake, low, high, back, out):
    pack = chosen(low, high)
    width = pack.shape[2]
    weight, head = split(pack[0, :width]), pack[0, width : width + 1]
    out[0] = back[0] + opponent(split(fake[0]), weight, head, scale)


def gen_kernel(scale, fake, pack, back, rows, gen, rows_chip, new_gen, made):
    weight, head = packed(pack)
    value = fake[0]
    total = back[0] + opponent(split(value), weight, head, scale)
    total = (1.0 - value * value) * total
    grad = scale * dot(split(rows[0]), split(total), (0, 0))
    gen_new = descend(gen[0], grad)
    new_gen[0] = gen_new
    made[0] = generated(split(rows_chip[0]), split(gen_new), scale)


def made_kernel(scale, new_gen, rows_far, low, high, far, first, last):
    cell = pl.program_id(0)
    gen = split(new_gen[0])
    far[0] = generated(split(rows_far[0]), gen, scale)
    edge = generated(split(chosen(low, high)[0]), gen, scale)

    @pl.when(cell == 0)
    def _():
        first[0] = edge

    @pl.when(cell == 1)
    def _():
        last[0] = edge


def near_kernel(scale, weight, head, real, rows, gen, gen_in, grad_w, grad_h):
    disc = split(weight[0])
    line = head[0]
    w, h = critic(real[0], disc, line, scale, True)
    rows = split(rows[0])
    for other in (gen, gen_in):
        made = generated(rows, split(other[0]), scale)
        more_w, more_h = critic(made, disc, line, scale, False)
        w, h = w + more_w, h + more_h
    grad_w[0] = w
    grad_h[0] = h


def chip_critic_kernel(scale, weight, head, made, grad_w, grad_h, out_w, out_h):
    w, h = critic(made[0], split(weight[0]), head[0], scale, False)
    out_w[0] = grad_w[0] + w
    out_h[0] = grad_h[0] + h


def outer_critic_kernel(scale, weight, head, low, high, grad_w, grad_h, out_w, out_h):
    w, h = critic(chosen(low, high)[0], split(weight[0]), head[0], scale, False)
    out_w[0] = grad_w[0] + w
    out_h[0] = grad_h[0] + h


def last_kernel(scale, weight, head, made, grad_w, grad_h, new_disc, new_head):
    w, h = critic(made[0], split(weight[0]), head[0], scale, False)
    new_disc[0] = descend(weight[0], grad_w[0] + w)
    new_head[0] = descend(head[0], grad_h[0] + h)


OWN, OTHER, FIXED = "own", "other", "fixed"
INDEX = {
    OWN: lambda cell: (cell, 0, 0),
    OTHER: lambda cell: (1 - cell, 0, 0),
    FIXED: lambda cell: (0, 0, 0),
}


def spec(array, kind):
    return pl.BlockSpec((1,) + array.shape[1:], INDEX[kind])


def call(body, inputs, outputs, products, name):
    count = 2
    arrays = [a for a, _ in inputs]
    size = sum(a.size * 4 for a in arrays) + sum(4 * s[0] * s[1] * s[2] for s, _ in outputs)
    outs = [jax.ShapeDtypeStruct(s, jnp.float32) for s, _ in outputs]
    return pl.pallas_call(
        body,
        grid=(count,),
        in_specs=[spec(a, k) for a, k in inputs],
        out_specs=[spec(o, k) for o, (_, k) in zip(outs, outputs)],
        out_shape=outs,
        name=name,
        cost_estimate=pl.CostEstimate(
            flops=products * 6 * 2 * 256 * 512 * 512, bytes_accessed=size, transcendentals=0
        ),
        compiler_params=pltpu.CompilerParams(
            dimension_semantics=("arbitrary",), vmem_limit_bytes=56 * 2**20
        ),
    )(*arrays)


def routes():
    nx, ny = lax.axis_size("gx"), lax.axis_size("gy")
    chip = [(i, i ^ 1) for i in range(ny)]
    far = [(i, (i + 1) % ny) for i in range(1, ny, 2)]
    far = far + [(b, a) for a, b in far]
    up = [(i, (i + 1) % nx) for i in range(nx)]
    down = [(b, a) for a, b in up]
    return chip, far, up, down


def local(samples, real_idx, latents, gen_weight, disc_weight, disc_head):
    cells, _, rows_n, width = latents.shape
    scale = width ** (-0.5)
    chip, far, up, down = routes()
    rows = latents.reshape(cells, rows_n, width)
    gen = gen_weight.reshape(cells, width, width)
    disc = disc_weight.reshape(cells, width, width)
    head = disc_head.reshape(cells, 1, width)

    def bind(kernel):
        return lambda *refs: kernel(scale, *refs)

    act = (cells, rows_n, width)
    edge = (1, rows_n, width)
    square = (cells, width, width)
    line = (cells, 1, width)

    pack, pack_first, pack_last = call(
        pack_kernel,
        [(disc, OWN), (head, OWN)],
        [
            ((cells, width + PAD, width), OWN),
            ((1, width + PAD, width), FIXED),
            ((1, width + PAD, width), FIXED),
        ],
        0,
        "pack",
    )
    pack_far = lax.ppermute(pack, "gy", far)
    pack_low = lax.ppermute(pack_last, "gx", up)
    pack_high = lax.ppermute(pack_first, "gx", down)
    pack_chip = lax.ppermute(pack, "gy", chip)
    rows_far = lax.ppermute(rows, "gy", far)
    rows_low = lax.ppermute(rows[1:], "gx", up)
    rows_high = lax.ppermute(rows[:1], "gx", down)
    rows_chip = lax.ppermute(rows, "gy", chip)

    fake, back = call(
        bind(start_kernel),
        [(rows, OWN), (gen, OWN), (disc, OWN), (head, OWN), (disc, OTHER), (head, OTHER)],
        [(act, OWN), (act, OWN)],
        5,
        "start",
    )
    (back,) = call(
        bind(chip_kernel), [(fake, OWN), (pack_chip, OWN), (back, OWN)], [(act, OWN)], 2, "chip"
    )
    (back,) = call(
        bind(outer_kernel),
        [(fake, OWN), (pack_low, FIXED), (pack_high, FIXED), (back, OWN)],
        [(act, OWN)],
        2,
        "outer",
    )
    new_gen, made_chip = call(
        bind(gen_kernel),
        [(fake, OWN), (pack_far, OWN), (back, OWN), (rows, OWN), (gen, OWN), (rows_chip, OWN)],
        [(square, OWN), (act, OWN)],
        4,
        "gen",
    )
    made_far, made_first, made_last = call(
        bind(made_kernel),
        [(new_gen, OWN), (rows_far, OWN), (rows_low, FIXED), (rows_high, FIXED)],
        [(act, OWN), (edge, FIXED), (edge, FIXED)],
        2,
        "made",
    )
    made_far = lax.ppermute(made_far, "gy", far)
    made_low = lax.ppermute(made_last, "gx", up)
    made_high = lax.ppermute(made_first, "gx", down)
    made_chip = lax.ppermute(made_chip, "gy", chip)

    real = jnp.take(samples, real_idx.reshape(-1), axis=0, mode="clip").reshape(act)
    grad_w, grad_h = call(
        bind(near_kernel),
        [
            (disc, OWN),
            (head, OWN),
            (real, OWN),
            (rows, OWN),
            (new_gen, OWN),
            (new_gen, OTHER),
        ],
        [(square, OWN), (line, OWN)],
        8,
        "near",
    )
    grad_w, grad_h = call(
        bind(chip_critic_kernel),
        [(disc, OWN), (head, OWN), (made_chip, OWN), (grad_w, OWN), (grad_h, OWN)],
        [(square, OWN), (line, OWN)],
        2,
        "critic_chip",
    )
    grad_w, grad_h = call(
        bind(outer_critic_kernel),
        [
            (disc, OWN),
            (head, OWN),
            (made_low, FIXED),
            (made_high, FIXED),
            (grad_w, OWN),
            (grad_h, OWN),
        ],
        [(square, OWN), (line, OWN)],
        2,
        "critic_outer",
    )
    new_disc, new_head = call(
        bind(last_kernel),
        [(disc, OWN), (head, OWN), (made_far, OWN), (grad_w, OWN), (grad_h, OWN)],
        [(square, OWN), (line, OWN)],
        2,
        "critic_far",
    )
    return (
        new_gen.reshape(gen_weight.shape),
        new_disc.reshape(disc_weight.shape),
        new_head.reshape(disc_head.shape),
    )


def solution(mesh):
    in_specs = (
        P(),
        P("gx", "gy", None),
        P("gx", "gy", None, None),
        P("gx", "gy", None, None),
        P("gx", "gy", None, None),
        P("gx", "gy", None),
    )
    out_specs = (P("gx", "gy", None, None), P("gx", "gy", None, None), P("gx", "gy", None))
    return jax.shard_map(local, mesh=mesh, in_specs=in_specs, out_specs=out_specs, check_vma=False)
```

```python
import math

import jax
import jax.numpy as jnp
from jax import lax
from jax.experimental import pallas as pl
from jax.experimental.pallas import tpu as pltpu
from jax.sharding import PartitionSpec as P


RATE = 0.25
LIMIT = 12
PAD = 8


def split(value):
    high = value.astype(jnp.bfloat16)
    low = (value - high.astype(jnp.float32)).astype(jnp.bfloat16)
    return high, low


def dot(left, right, dims):
    def one(a, b):
        return lax.dot_general(
            a, b, ((dims[:1], dims[1:]), ((), ())), preferred_element_type=jnp.float32
        )

    return one(left[0], right[0]) + (one(left[0], right[1]) + one(left[1], right[0]))


def generated(rows, weight, scale):
    return jnp.tanh(scale * dot(rows, weight, (1, 0)))


def opponent(fake, weight, head, scale):
    hidden = jnp.tanh(scale * dot(fake, weight, (1, 0)))
    score = scale * jnp.sum(hidden * head, axis=1, keepdims=True)
    slope = -jax.nn.sigmoid(-score)
    inner = (1.0 - hidden * hidden) * ((scale * slope) * head)
    return scale * dot(split(inner), weight, (1, 1))


def critic(rows, weight, head, scale, real_side):
    rows = split(rows)
    hidden = jnp.tanh(scale * dot(rows, weight, (1, 0)))
    score = scale * jnp.sum(hidden * head, axis=1, keepdims=True)
    if real_side:
        slope = -jax.nn.sigmoid(-score)
    else:
        slope = 0.2 * jax.nn.sigmoid(score)
    inner = (1.0 - hidden * hidden) * ((scale * slope) * head)
    grad_w = scale * dot(rows, split(inner), (0, 0))
    grad_h = scale * jnp.sum(slope * hidden, axis=0, keepdims=True)
    return grad_w, grad_h


def descend(value, grad):
    mean_sq = jnp.mean(grad * grad)
    return value - RATE * grad * lax.rsqrt(mean_sq + 1e-06)


def fill(out, weight, head):
    width = weight.shape[1]
    out[0, :width] = weight[0]
    out[0, width:] = jnp.broadcast_to(head[0], (PAD, width))


def pack_kernel(cell, flags, weight, head, both, first, last, edge):
    fill(both, weight, head)

    @pl.when(cell == 0)
    def _():
        fill(first, weight, head)

    @pl.when(cell == 1)
    def _():
        fill(last, weight, head)

    @pl.when(cell == flags[1])
    def _():
        fill(edge, weight, head)


def rows_kernel(cell, flags, rows, first, last, edge):
    @pl.when(cell == 0)
    def _():
        first[...] = rows[...]

    @pl.when(cell == 1)
    def _():
        last[...] = rows[...]

    @pl.when(cell == flags[1])
    def _():
        edge[...] = rows[...]


def start_kernel(scale, cell, rows, gen, weight, head, weight_in, head_in, fake, back):
    value = generated(split(rows[0]), split(gen[0]), scale)
    fake[0] = value
    value = split(value)
    total = opponent(value, split(weight[0]), head[0], scale)
    back[0] = total + opponent(value, split(weight_in[0]), head_in[0], scale)


def packed(ref):
    width = ref.shape[2]
    return split(ref[0, :width]), ref[0, width : width + 1]


def chip_kernel(scale, cell, fake, pack, back, out):
    weight, head = packed(pack)
    out[0] = back[0] + opponent(split(fake[0]), weight, head, scale)


def chosen(cell, low, high):
    return jnp.where(cell == 0, low[...], high[...])


def relayed(cell, flags, low, high, relay):
    value = jnp.where(cell == 0, low[0], high[0])
    return jnp.where(flags[cell] == 1, relay[0], value)


def outer_kernel(scale, cell, flags, fake, low, high, relay, back, out):
    width = low.shape[2]
    pack = relayed(cell, flags, low, high, relay)
    weight, head = split(pack[:width]), pack[width : width + 1]
    out[0] = back[0] + opponent(split(fake[0]), weight, head, scale)


def gen_kernel(scale, cell, fake, pack, back, rows, gen, new_gen, gen_out):
    weight, head = packed(pack)
    value = fake[0]
    total = back[0] + opponent(split(value), weight, head, scale)
    total = (1.0 - value * value) * total
    grad = scale * dot(split(rows[0]), split(total), (0, 0))
    gen_new = descend(gen[0], grad)
    new_gen[0] = gen_new
    gen_out[0] = gen_new


def edge_kernel(scale, cell, flags, new_gen, rows_chip, low, high, relay, made, first, last):
    gen = split(new_gen[0])
    made[0] = generated(split(rows_chip[0]), gen, scale)
    value = generated(split(relayed(cell, flags, low, high, relay)), gen, scale)

    @pl.when(cell == 0)
    def _():
        first[0] = value

    @pl.when(cell == 1)
    def _():
        last[0] = value


def far_kernel(scale, cell, new_gen, rows_far, far):
    far[0] = generated(split(rows_far[0]), split(new_gen[0]), scale)


def real_kernel(scale, cell, index, weight, head, table, grad_w, grad_h, real):
    def pick(row, _):
        real[pl.ds(row, 1)] = table[pl.ds(index[cell, row], 1)]
        return 0

    lax.fori_loop(0, real.shape[0], pick, 0, unroll=8)
    w, h = critic(real[...], split(weight[0]), head[0], scale, True)
    grad_w[0] = w
    grad_h[0] = h


def near_kernel(scale, cell, weight, head, rows, gen, gen_in, in_w, in_h, grad_w, grad_h):
    disc = split(weight[0])
    line = head[0]
    rows = split(rows[0])
    w, h = in_w[0], in_h[0]
    for other in (gen, gen_in):
        made = generated(rows, split(other[0]), scale)
        more_w, more_h = critic(made, disc, line, scale, False)
        w, h = w + more_w, h + more_h
    grad_w[0] = w
    grad_h[0] = h


def chip_critic_kernel(scale, cell, weight, head, made, grad_w, grad_h, out_w, out_h):
    w, h = critic(made[0], split(weight[0]), head[0], scale, False)
    out_w[0] = grad_w[0] + w
    out_h[0] = grad_h[0] + h


def outer_critic_kernel(scale, cell, weight, head, low, high, grad_w, grad_h, out_w, out_h):
    w, h = critic(chosen(cell, low, high)[0], split(weight[0]), head[0], scale, False)
    out_w[0] = grad_w[0] + w
    out_h[0] = grad_h[0] + h


def last_kernel(scale, cell, weight, head, made, grad_w, grad_h, new_disc, new_head):
    w, h = critic(made[0], split(weight[0]), head[0], scale, False)
    new_disc[0] = descend(weight[0], grad_w[0] + w)
    new_head[0] = descend(head[0], grad_h[0] + h)


OWN, OTHER, FIXED = "own", "other", "fixed"
KEEP = True


def view(ref, kind, cell):
    if kind == OWN:
        return ref.at[pl.ds(cell, 1)]
    if kind == OTHER:
        return ref.at[pl.ds(1 - cell, 1)]
    return ref


def inside(value):
    if jax.typeof(value).memory_space == pltpu.VMEM:
        return value
    return pltpu.with_memory_space_constraint(value, pltpu.VMEM)


def call(body, inputs, outputs, products, scalars=None, scratch=()):
    arrays = [inside(a) for a, _ in inputs]
    kinds = [k for _, k in inputs] + [o[1] for o in outputs]
    size = sum(a.size * 4 for a in arrays) + sum(4 * math.prod(o[0]) for o in outputs)
    extra = [] if scalars is None else [scalars]

    def kernel(*refs):
        front, refs = refs[: len(extra)], refs[len(extra) :]

        @pl.loop(0, 2)
        def _(cell):
            views = [view(r, k, cell) for r, k in zip(refs, kinds)]
            body(cell, *front, *views, *refs[len(kinds) :])

    return pl.pallas_call(
        kernel,
        in_specs=[pl.BlockSpec(memory_space=pltpu.SMEM)] * len(extra)
        + [pl.BlockSpec(memory_space=pltpu.VMEM)] * len(inputs),
        out_specs=[pl.BlockSpec(memory_space=pltpu.VMEM)] * len(outputs),
        out_shape=[
            pltpu.VMEM(o[0], jnp.float32)
            if len(o) == 3
            else jax.ShapeDtypeStruct(o[0], jnp.float32)
            for o in outputs
        ],
        scratch_shapes=scratch,
        cost_estimate=pl.CostEstimate(
            flops=products * 6 * 2 * 256 * 512 * 512, bytes_accessed=size, transcendentals=0
        ),
        compiler_params=pltpu.CompilerParams(vmem_limit_bytes=LIMIT * 2**20),
    )(*extra, *arrays)


AXES = ("gx", "gy")
LINE = 4


def routes():
    nx, ny = lax.axis_size("gx"), lax.axis_size("gy")
    chip = [(i, i ^ 1) for i in range(ny)]
    far = [(i, (i + 1) % ny) for i in range(1, ny, 2)]
    far = far + [(b, a) for a, b in far]
    up = [(i, (i + 1) % nx) for i in range(nx)]
    down = [(b, a) for a, b in up]
    return chip, far, up, down


def relays():
    nx, ny = lax.axis_size("gx"), lax.axis_size("gy")

    def flat(pairs, odd):
        return [(a * ny + j, b * ny + j) for a, b in pairs for j in range(ny) if j % 2 in odd]

    inner = [(i, i + 1) for i in range(nx) if i % LINE != LINE - 1]
    wrap = [(i, (i + 1) % nx) for i in range(LINE - 1, nx, LINE)]
    part = flat(inner, (0, 1)) + flat(wrap, (0,))
    hops = [(a, (b + 2) % nx, b) for a, b in wrap] + [(b, (a - 2) % nx, a) for a, b in wrap]
    leave = [(a, m) for a, m, _ in hops]
    enter = [(m, b) for _, m, b in hops]

    def back(pairs):
        return [(b, a) for a, b in pairs]

    return (part, back(part), flat(leave, (1,)), flat(enter, (1,))), (
        inner,
        back(inner),
        leave,
        enter,
    )


def local(samples, real_idx, latents, gen_weight, disc_weight, disc_head):
    cells, _, rows_n, width = latents.shape
    scale = width ** (-0.5)
    chip, far, up, down = routes()
    disc_routes, rows_routes = relays()
    place = lax.axis_index("gx") % LINE
    odd = lax.axis_index("gy") % 2
    ends = jnp.stack([place == 0, place == LINE - 1]).astype(jnp.int32)
    odd_ends = ends * odd
    rows = latents.reshape(cells, rows_n, width)
    gen = gen_weight.reshape(cells, width, width)
    disc = disc_weight.reshape(cells, width, width)
    head = disc_head.reshape(cells, 1, width)

    def bind(kernel):
        return lambda cell, *refs: kernel(scale, cell, *refs)

    act = (cells, rows_n, width)
    edge = (1, rows_n, width)
    square = (cells, width, width)
    line = (cells, 1, width)

    tall = width + PAD
    pack, pack_first, pack_last, pack_edge = call(
        pack_kernel,
        [(disc, OWN), (head, OWN)],
        [((cells, tall, width), OWN)] + [((1, tall, width), FIXED)] * 3,
        0,
        scalars=ends,
    )
    pack_far = lax.ppermute(pack, "gy", far)
    pack_mid = lax.ppermute(pack_edge, AXES, disc_routes[2])
    pack_low = lax.ppermute(pack_last, AXES, disc_routes[0])
    pack_high = lax.ppermute(pack_first, AXES, disc_routes[1])
    pack_chip = lax.ppermute(pack, "gy", chip)
    pack_mid = lax.ppermute(pack_mid, AXES, disc_routes[3])

    rows_first, rows_last, rows_edge = call(
        rows_kernel, [(rows, OWN)], [(edge, FIXED)] * 3, 0, scalars=ends
    )
    rows_far = lax.ppermute(rows, "gy", far)
    rows_mid = lax.ppermute(rows_edge, "gx", rows_routes[2])
    rows_low = lax.ppermute(rows_last, "gx", rows_routes[0])
    rows_high = lax.ppermute(rows_first, "gx", rows_routes[1])
    rows_chip = lax.ppermute(rows, "gy", chip)
    rows_mid = lax.ppermute(rows_mid, "gx", rows_routes[3])

    fake, back = call(
        bind(start_kernel),
        [(rows, OWN), (gen, OWN), (disc, OWN), (head, OWN), (disc, OTHER), (head, OTHER)],
        [(act, OWN, KEEP), (act, OWN, KEEP)],
        5,
    )
    (back,) = call(
        bind(chip_kernel), [(fake, OWN), (pack_chip, OWN), (back, OWN)], [(act, OWN, KEEP)], 2
    )
    table = samples.reshape((1,) + samples.shape)
    grad_w, grad_h = call(
        lambda cell, *refs: real_kernel(
            scale, cell, *refs[:3], refs[3].at[0], *refs[4:]
        ),
        [(disc, OWN), (head, OWN), (table, FIXED)],
        [(square, OWN, KEEP), (line, OWN, KEEP)],
        2,
        scalars=real_idx.reshape(cells, rows_n),
        scratch=[pltpu.VMEM((rows_n, width), jnp.float32)],
    )
    (back,) = call(
        bind(outer_kernel),
        [(fake, OWN), (pack_low, FIXED), (pack_high, FIXED), (pack_mid, FIXED), (back, OWN)],
        [(act, OWN, KEEP)],
        2,
        scalars=odd_ends,
    )
    new_gen, gen_out = call(
        bind(gen_kernel),
        [(fake, OWN), (pack_far, OWN), (back, OWN), (rows, OWN), (gen, OWN)],
        [(square, OWN, KEEP), (square, OWN)],
        3,
    )
    made_chip, made_first, made_last = call(
        bind(edge_kernel),
        [
            (new_gen, OWN),
            (rows_chip, OWN),
            (rows_low, FIXED),
            (rows_high, FIXED),
            (rows_mid, FIXED),
        ],
        [(act, OWN), (edge, FIXED), (edge, FIXED)],
        2,
        scalars=ends,
    )
    (made_far,) = call(bind(far_kernel), [(new_gen, OWN), (rows_far, OWN)], [(act, OWN)], 1)
    made_far = lax.ppermute(made_far, "gy", far)
    made_low = lax.ppermute(made_last, "gx", up)
    made_high = lax.ppermute(made_first, "gx", down)
    made_chip = lax.ppermute(made_chip, "gy", chip)

    grad_w, grad_h = call(
        bind(near_kernel),
        [
            (disc, OWN),
            (head, OWN),
            (rows, OWN),
            (new_gen, OWN),
            (new_gen, OTHER),
            (grad_w, OWN),
            (grad_h, OWN),
        ],
        [(square, OWN, KEEP), (line, OWN, KEEP)],
        6,
    )
    grad_w, grad_h = call(
        bind(outer_critic_kernel),
        [
            (disc, OWN),
            (head, OWN),
            (made_low, FIXED),
            (made_high, FIXED),
            (grad_w, OWN),
            (grad_h, OWN),
        ],
        [(square, OWN, KEEP), (line, OWN, KEEP)],
        2,
    )
    grad_w, grad_h = call(
        bind(chip_critic_kernel),
        [(disc, OWN), (head, OWN), (made_chip, OWN), (grad_w, OWN), (grad_h, OWN)],
        [(square, OWN, KEEP), (line, OWN, KEEP)],
        2,
    )
    new_disc, new_head = call(
        bind(last_kernel),
        [(disc, OWN), (head, OWN), (made_far, OWN), (grad_w, OWN), (grad_h, OWN)],
        [(square, OWN), (line, OWN)],
        2,
    )
    return (
        gen_out.reshape(gen_weight.shape),
        new_disc.reshape(disc_weight.shape),
        new_head.reshape(disc_head.shape),
    )


def solution(mesh):
    in_specs = (
        P(),
        P("gx", "gy", None),
        P("gx", "gy", None, None),
        P("gx", "gy", None, None),
        P("gx", "gy", None, None),
        P("gx", "gy", None),
    )
    out_specs = (P("gx", "gy", None, None), P("gx", "gy", None, None), P("gx", "gy", None))

    return jax.shard_map(local, mesh=mesh, in_specs=in_specs, out_specs=out_specs, check_vma=False)
```
